32 devices in a mesh: groups: 2 (over y), ctx: 4 (over z), tp: 4 (over x, core).
Axes of the slice: x: 2, y: 2, z: 4, core: 2. Of those that a mesh axis runs over, the one named last changes fastest.
Arguments:
- x_in: bfloat16 [4096, 4096], P(('groups', 'ctx'), 'tp'), parts along dimension 0, may hold values from -6 to 6
- z_in: bfloat16 [4096, 4096], P(('groups', 'ctx'), 'tp'), parts along dimension 0, may hold values from -6 to 6
- b_in: bfloat16 [4096, 512], P(('groups', 'ctx'), 'tp'), parts along dimension 0, may hold values from -6 to 6
- c_in: bfloat16 [4096, 512], P(('groups', 'ctx'), 'tp'), parts along dimension 0, may hold values from -6 to 6
- dt_in: bfloat16 [4096, 64], P(('groups', 'ctx'), 'tp'), parts along dimension 0, may hold values from -4 to 14
- conv_x: bfloat16 [4, 4096], P(None, 'tp'), may hold values from -3 to 3
- conv_bc: bfloat16 [2, 4, 512], P(None, None, 'tp'), may hold values from -3 to 3
- dt_bias: float32 [64], P('tp'), may hold values from -13 to -2
- a_log: float32 [64], P('tp'), may hold values from -0.7 to 0.4
- d_skip: float32 [64], P('tp'), may hold values from 0.5 to 1.5
- norm_gain: bfloat16 [4096], P('tp'), may hold values from 0.5 to 1.5
- out_weight: bfloat16 [4096, 4096], P('ctx', 'tp'), may hold values from -0.09375 to 0.09375
Outputs:
- mixed: bfloat16 [4096, 4096], P(('groups', 'ctx'), 'tp'), parts along dimension 0
The draws below stay inside these ranges and needn't reach their ends.
There are 2 independent parts, one for each index of `groups`. The reference program is written for one: setup_inputs(seed, part) draws one part's arguments, and reference() takes and returns one part's arrays. A program takes and returns all parts, laid end to end along the dimension named above; an argument that names none is the same for every part. Nothing has to cross between parts.
All inputs are finite; a program needn't handle non-finite values.
Results may differ from the reference program's by a relative error of at most 0.0059.
Values may be sent and summed in bfloat16 or wider, within the bound.
No kernel may reach another device: no remote copies, remote signals or barrier semaphores. Data moves between devices by JAX's collectives and lax.ppermute only.
A program may use at most 128 MiB of HBM per device.

```python
import math
import jax
import jax.numpy as jnp
from jax import lax

HEADS = 64
HEAD_DIM = 64
STATE = 128
GROUPS = 4
OUT_WIDTH = 4096
SPAN = 256
CONV_WIDTH = 4
INNER = 4096
TOKENS = 2048


def draw_dt_bias(key, part):
    key_class, key_slow, key_fast = jax.random.split(key, 3)
    picked = jax.random.uniform(key_class, (HEADS,))
    share = 0.5
    slow_value = -math.log(float(TOKENS)) + jax.random.uniform(key_slow, (HEADS,), minval=-0.3, maxval=0.3)
    fast_value = jax.random.uniform(key_fast, (HEADS,), minval=-4.0, maxval=-3.0)
    return jnp.where(picked < share, slow_value, fast_value).astype(jnp.float32)


def draw_dt_in(key, part):
    key_noise, key_offset, key_spots = jax.random.split(key, 3)
    noise = 0.5 * jax.random.normal(key_noise, (TOKENS, HEADS))
    offsets = jax.random.uniform(key_offset, (TOKENS // SPAN, 1, HEADS), minval=-0.7, maxval=0.7)
    offsets = jnp.broadcast_to(offsets, (TOKENS // SPAN, SPAN, HEADS)).reshape(TOKENS, HEADS)
    spots = jax.random.randint(key_spots, (6,), 0, TOKENS)
    struck = jnp.any(jnp.arange(TOKENS)[:, None] == spots[None, :], axis=1)
    jump_size = math.log(0.4 * TOKENS)
    raw_value = noise + offsets + jnp.where(struck[:, None], jump_size, 0.0)
    return jnp.clip(raw_value, -4.0, 14.0).astype(jnp.float32).astype(jnp.bfloat16)


def block_levels(stream_key, extent, cuts, least, largest):
    level, own = 1.0, jax.random.fold_in(stream_key, 6)
    for axis_at, shards_of in cuts:
        steps = jnp.exp(jax.random.uniform(jax.random.fold_in(own, axis_at), (shards_of,), jnp.float32, least / len(cuts), largest / len(cuts)))
        level = level * jnp.repeat(steps, extent[axis_at] // shards_of).reshape([-1 if axis == axis_at else 1 for axis in range(len(extent))])
    return level


def bell_draw(rng, shape, deviation, most, pieces=(), kind=jnp.bfloat16):
    loudness = block_levels(rng, shape, pieces, -0.22, 0.18) if pieces else 1.0
    entries = jax.random.normal(rng, shape, jnp.float32) * deviation * loudness
    return jnp.minimum(jnp.maximum(entries, -most), most).astype(kind)


def setup_inputs(seed: int = 0, part: int = 0) -> dict:
    seeds = jax.random.split(jax.random.key(seed), 13)
    own_keys = jax.random.split(jax.random.fold_in(seeds[12], part), 13)
    return {
        "x_in": bell_draw(own_keys[0], (TOKENS, INNER), 1.0, 6.0, ((0, 4), (1, 4))),
        "z_in": bell_draw(own_keys[1], (TOKENS, INNER), 1.0, 6.0, ((0, 4), (1, 4))),
        "b_in": bell_draw(own_keys[2], (TOKENS, GROUPS * STATE), 1.0, 6.0, ((0, 4), (1, 4))),
        "c_in": bell_draw(own_keys[3], (TOKENS, GROUPS * STATE), 1.0, 6.0, ((0, 4), (1, 4))),
        "dt_in": draw_dt_in(jax.random.fold_in(jax.random.fold_in(seeds[12], part), 71), part),
        "conv_x": bell_draw(seeds[5], (CONV_WIDTH, INNER), CONV_WIDTH ** -0.5, 3.0, ((1, 4),)),
        "conv_bc": bell_draw(seeds[6], (2, CONV_WIDTH, GROUPS * STATE), CONV_WIDTH ** -0.5, 3.0, ((2, 4),)),
        "dt_bias": draw_dt_bias(jax.random.fold_in(seeds[12], 71), part),
        "a_log": jnp.clip(-0.7 + 1.1 * jax.random.uniform(seeds[8], (HEADS,), jnp.float32) ** block_levels(seeds[8], (HEADS,), ((0, 4),), -0.2, 0.2), -0.7, 0.4),
        "d_skip": jnp.clip(0.5 + 1.0 * jax.random.uniform(seeds[9], (HEADS,), jnp.float32) ** block_levels(seeds[9], (HEADS,), ((0, 4),), -0.2, 0.2), 0.5, 1.5),
        "norm_gain": jnp.clip(1.0 + 0.1 * jax.random.normal(seeds[10], (INNER,), jnp.float32), 0.5, 1.5).astype(jnp.bfloat16),
        "out_weight": bell_draw(seeds[11], (INNER, OUT_WIDTH), INNER ** -0.5, 0.09375, ((0, 4), (1, 4))),
    }


EPS = 1e-05

def causal_conv(extended, taps, length):
    summed = jnp.zeros((length, extended.shape[1]), jnp.float32)
    for kernel_tap in range(taps.shape[0]):
        summed = summed + extended[kernel_tap:kernel_tap + length].astype(jnp.float32) * taps[kernel_tap].astype(jnp.float32)
    return jax.nn.silu(summed).astype(jnp.bfloat16)

def span_parts(x_rows, b_rows, c_rows, step_span, decay_rate, groups, widen):
    length = x_rows.shape[0]
    head_count = step_span.shape[1]
    per_group = head_count // groups
    state_size = b_rows.shape[1] // groups
    b_groups = b_rows.reshape(length, groups, state_size)
    c_groups = c_rows.reshape(length, groups, state_size)
    x_heads = x_rows.reshape(length, head_count, -1)
    cumulative = jnp.cumsum(step_span * decay_rate[None, :], axis=0)
    if widen:
        scores = jnp.einsum('tgn,sgn->gts', c_groups.astype(jnp.float32), b_groups.astype(jnp.float32))
    else:
        scores = jnp.einsum('tgn,sgn->gts', c_groups, b_groups, preferred_element_type=jnp.float32)
    positions = jnp.arange(length)
    causal = positions[:, None] >= positions[None, :]
    transposed = cumulative.T
    gaps = jnp.where(causal[None], transposed[:, :, None] - transposed[:, None, :], -1e+30)
    mixing = (jnp.repeat(scores, per_group, axis=0) * jnp.exp(gaps) * step_span.T[:, None, :]).astype(jnp.bfloat16)
    if widen:
        diagonal_part = jnp.einsum('hts,shp->thp', mixing.astype(jnp.float32), x_heads.astype(jnp.float32))
    else:
        diagonal_part = jnp.einsum('hts,shp->thp', mixing, x_heads, preferred_element_type=jnp.float32)
    to_end = jnp.exp(cumulative[-1][None, :] - cumulative) * step_span
    weighted = (x_heads.astype(jnp.float32) * to_end[:, :, None]).astype(jnp.bfloat16)
    b_heads = jnp.repeat(b_groups, per_group, axis=1)
    if widen:
        local_state = jnp.einsum('shp,shn->hpn', weighted.astype(jnp.float32), b_heads.astype(jnp.float32))
    else:
        local_state = jnp.einsum('shp,shn->hpn', weighted, b_heads, preferred_element_type=jnp.float32)
    return (diagonal_part.reshape(length, -1), local_state, cumulative)

def carried(c_rows, cumulative, entering, groups):
    length = c_rows.shape[0]
    head_count = cumulative.shape[1]
    state_size = entering.shape[2]
    c_heads = jnp.repeat(c_rows.reshape(length, groups, state_size), head_count // groups, axis=1).astype(jnp.float32)
    summed = jnp.einsum('thn,hpn->thp', c_heads, entering, precision=lax.Precision.HIGHEST)
    return (summed * jnp.exp(cumulative)[:, :, None]).reshape(length, -1)

def finish(ssd_part, x_rows, gate_rows, d_skip, norm_gain, groups):
    length, inner_here = x_rows.shape
    head_count = d_skip.shape[0]
    skip_term = (x_rows.astype(jnp.float32).reshape(length, head_count, -1) * d_skip[None, :, None]).reshape(length, inner_here)
    gated = (ssd_part + skip_term) * jax.nn.silu(gate_rows.astype(jnp.float32))
    grouped = gated.reshape(length, groups, -1)
    scale = lax.rsqrt(lax.optimization_barrier(jnp.mean(grouped * grouped, axis=2, keepdims=True)) + EPS)
    return ((grouped * scale).reshape(length, inner_here) * norm_gain.astype(jnp.float32)).astype(jnp.bfloat16)

def reference(x_in, z_in, b_in, c_in, dt_in, conv_x, conv_bc, dt_bias, a_log, d_skip, norm_gain, out_weight):
    rim_rows = CONV_WIDTH - 1
    xs = causal_conv(jnp.concatenate([jnp.zeros((rim_rows, x_in.shape[1]), jnp.bfloat16), x_in], 0), conv_x, TOKENS)
    bs = causal_conv(jnp.concatenate([jnp.zeros((rim_rows, b_in.shape[1]), jnp.bfloat16), b_in], 0), conv_bc[0], TOKENS)
    cs = causal_conv(jnp.concatenate([jnp.zeros((rim_rows, c_in.shape[1]), jnp.bfloat16), c_in], 0), conv_bc[1], TOKENS)
    step_size = jax.nn.softplus(dt_in.astype(jnp.float32) + dt_bias[None, :])
    decay_rate = -jnp.exp(a_log)

    def advance(entering, span_index):
        first_row = (span_index * SPAN).astype(jnp.int32)

        def take_rows(array):
            return lax.dynamic_slice_in_dim(array, first_row, SPAN, 0)
        c_rows = take_rows(cs)
        x_rows = take_rows(xs)
        diagonal_part, local_state, cumulative = span_parts(x_rows, take_rows(bs), c_rows, take_rows(step_size), decay_rate, GROUPS, True)
        ssd_part = diagonal_part + carried(c_rows, cumulative, entering, GROUPS)
        following = jnp.exp(cumulative[-1])[:, None, None] * entering + local_state
        return (following, finish(ssd_part, x_rows, take_rows(z_in), d_skip, norm_gain, GROUPS))
    start_state = jnp.zeros((HEADS, HEAD_DIM, STATE), jnp.float32)
    unused, normed = lax.scan(advance, start_state, jnp.arange(TOKENS // SPAN, dtype=jnp.int32))
    normed = normed.reshape(TOKENS, INNER)
    return jnp.dot(normed, out_weight, preferred_element_type=jnp.float32).astype(jnp.bfloat16)
```

```python
import functools
import jax
import jax.numpy as jnp
from jax import lax
from jax.experimental import pallas as pl
from jax.experimental.pallas import tpu as pltpu
from jax.sharding import PartitionSpec as P

STATE = 128
SPAN = 256
HALF = 128
EPS = 1e-05
LOG2E = 1.4426950408889634
F32 = jnp.float32
BF16 = jnp.bfloat16
HI = lax.Precision.HIGHEST
VMEM = pl.BlockSpec(memory_space=pltpu.VMEM)
SMEM = pl.BlockSpec(memory_space=pltpu.SMEM)
ANY = pl.BlockSpec(memory_space=pl.ANY)


def params():
    return pltpu.CompilerParams(vmem_limit_bytes=48 * 1024 * 1024)


def pair_lanes(rows, left):
    return lax.broadcasted_iota(jnp.int32, (rows, 2 * left), 1) < left


def spread(table, pair, mask):
    rows, lanes = mask.shape
    first = jnp.broadcast_to(table[:, 2 * pair : 2 * pair + 1], (rows, lanes))
    second = jnp.broadcast_to(table[:, 2 * pair + 1 : 2 * pair + 2], (rows, lanes))
    return jnp.where(mask, first, second)


def conv_states_kernel(
    x_ref, b_ref, c_ref, halo_ref, dt_ref, taps_ref, bias_ref, alog_ref,
    xbc_ref, cum_ref, lstep_ref, first_ref, msg_ref, ext,
):
    length, inner = x_ref.shape
    heads = dt_ref.shape[1]
    spans = length // SPAN
    width = ext.shape[1]
    chunk = 128
    ext[0:8, :] = halo_ref[...].astype(F32)
    ext[8:, 0:inner] = x_ref[...].astype(F32)
    ext[8:, inner : inner + STATE] = b_ref[...].astype(F32)
    ext[8:, inner + STATE :] = c_ref[...].astype(F32)
    taps_count = taps_ref.shape[0]
    for col in range(0, width, 128):
        taps = taps_ref[:, col : col + 128]
        for row in range(0, length, chunk):
            total = jnp.zeros((chunk, 128), F32)
            for k in range(taps_count):
                start = 8 - (taps_count - 1) + k + row
                total = total + ext[start : start + chunk, col : col + 128] * taps[k : k + 1]
            xbc_ref[row : row + chunk, col : col + 128] = (
                total * lax.logistic(total)
            ).astype(BF16)
    value = dt_ref[...].astype(F32) + bias_ref[...]
    step = jnp.maximum(value, 0.0) + jnp.log1p(jnp.exp(-jnp.abs(value)))
    log_decay = step * (-jnp.exp(alog_ref[...]) * LOG2E)
    lstep_ref[...] = jnp.log2(step)
    tri = (
        lax.broadcasted_iota(jnp.int32, (SPAN, SPAN), 0)
        >= lax.broadcasted_iota(jnp.int32, (SPAN, SPAN), 1)
    ).astype(F32)
    head_dim = inner // heads
    mask = pair_lanes(SPAN, head_dim)
    row_mask = pair_lanes(8, head_dim)
    cums, ends = [], []
    for k in range(spans):
        rows = slice(k * SPAN, (k + 1) * SPAN)
        cum = jnp.dot(tri, log_decay[rows], precision=HI, preferred_element_type=F32)
        cum_ref[rows, :] = cum
        last = cum[SPAN - 1 : SPAN]
        cums.append(last)
        ends.append(jnp.exp2(last - cum) * step[rows])
    total_log = cums[0]
    for k in range(1, spans):
        total_log = total_log + cums[k]
    for pair in range(heads // 2):
        cols = slice(pair * 128, (pair + 1) * 128)
        state = None
        for k in range(spans):
            rows = slice(k * SPAN, (k + 1) * SPAN)
            weighted = (
                xbc_ref[rows, cols].astype(F32) * spread(ends[k], pair, mask)
            ).astype(BF16)
            local = lax.dot_general(
                xbc_ref[rows, inner : inner + STATE], weighted,
                (((0,), (0,)), ((), ())), preferred_element_type=F32,
            )
            if state is None:
                state = local
                first_ref[:, cols] = local.astype(BF16)
            else:
                decay = spread(jnp.broadcast_to(jnp.exp2(cums[k]), (8, heads)), pair, row_mask)
                state = decay[0:1] * state + local
        msg_ref[0:STATE, cols] = state.astype(BF16)
        gone = spread(jnp.broadcast_to(jnp.exp2(total_log), (8, heads)), pair, row_mask)
        high = gone.astype(BF16)
        low = (gone - high.astype(F32)).astype(BF16)
        msg_ref[STATE : STATE + 8, cols] = high
        msg_ref[STATE + 8 : STATE + 16, cols] = low


def diagonal_kernel(xbc_ref, cum_ref, lstep_ref, first_ref, skip_ref, acc_ref):
    length, inner = acc_ref.shape
    heads = cum_ref.shape[1]
    spans = length // SPAN
    head_dim = inner // heads
    mask = pair_lanes(SPAN, head_dim)
    half_mask = pair_lanes(HALF, head_dim)
    rows_i = lax.broadcasted_iota(jnp.int32, (SPAN, SPAN), 0)
    cols_i = lax.broadcasted_iota(jnp.int32, (SPAN, SPAN), 1)
    eye = (rows_i == cols_i).astype(F32)
    for k in range(spans):
        rows = slice(k * SPAN, (k + 1) * SPAN)
        cum = cum_ref[rows, :]
        back = lax.dot_general(
            cum - lstep_ref[rows, :], eye, (((0,), (0,)), ((), ())),
            precision=HI, preferred_element_type=F32,
        )
        b_span = xbc_ref[rows, inner : inner + STATE]
        c_span = xbc_ref[rows, inner + STATE :]
        scores = lax.dot_general(
            c_span, b_span, (((1,), (1,)), ((), ())), preferred_element_type=F32
        )
        scores = jnp.where(rows_i >= cols_i, scores, 0.0)
        if k:
            grown = jnp.exp2(cum)
        for pair in range(heads // 2):
            cols = slice(pair * 128, (pair + 1) * 128)
            x_pair = xbc_ref[rows, cols]
            tops, lows = [], []
            for h in (2 * pair, 2 * pair + 1):
                later = jnp.broadcast_to(cum[:, h : h + 1], (SPAN, HALF))
                row0 = back[h : h + 1, 0:HALF]
                row1 = back[h : h + 1, HALF:]
                m00 = scores[0:HALF, 0:HALF] * jnp.exp2(jnp.minimum(later[0:HALF] - row0, 100.0))
                m10 = scores[HALF:, 0:HALF] * jnp.exp2(later[HALF:] - row0)
                m11 = scores[HALF:, HALF:] * jnp.exp2(jnp.minimum(later[HALF:] - row1, 100.0))
                tops.append(jnp.dot(m00.astype(BF16), x_pair[0:HALF], preferred_element_type=F32))
                lows.append(
                    jnp.dot(
                        jnp.concatenate([m10.astype(BF16), m11.astype(BF16)], axis=1),
                        x_pair, preferred_element_type=F32,
                    )
                )
            top = jnp.where(half_mask, tops[0], tops[1])
            low = jnp.where(half_mask, lows[0], lows[1])
            skip = jnp.where(half_mask, skip_ref[2 * pair], skip_ref[2 * pair + 1])
            x_f = x_pair.astype(F32)
            top = top + skip * x_f[0:HALF]
            low = low + skip * x_f[HALF:]
            if k:
                inner_state = jnp.dot(c_span, first_ref[:, cols], preferred_element_type=F32)
                term = inner_state * spread(grown, pair, mask)
                top = top + term[0:HALF]
                low = low + term[HALF:]
            acc_ref[k * SPAN : k * SPAN + HALF, cols] = top
            acc_ref[k * SPAN + HALF : (k + 1) * SPAN, cols] = low


def finish_kernel(acc_ref, xbc_ref, cum_ref, z_ref, near_ref, far_ref, gain_ref, out_ref, gated):
    length, inner = acc_ref.shape
    heads = cum_ref.shape[1]
    head_dim = inner // heads
    chunk = 128
    mask = pair_lanes(chunk, head_dim)
    decay = near_ref[STATE : STATE + 1, :].astype(F32) + near_ref[STATE + 8 : STATE + 9, :].astype(F32)
    entering = (
        near_ref[0:STATE, :].astype(F32) + decay * far_ref[...].astype(F32)
    ).astype(BF16)
    offset = jnp.zeros((1, heads), F32)
    for row in range(0, length, chunk):
        rows = slice(row, row + chunk)
        if row and row % SPAN == 0:
            offset = offset + cum_ref[row - 1 : row, :]
        grown = jnp.exp2(cum_ref[rows, :] + offset)
        c_rows = xbc_ref[rows, inner + STATE :]
        squares = jnp.zeros((chunk, 128), F32)
        for pair in range(heads // 2):
            cols = slice(pair * 128, (pair + 1) * 128)
            term = jnp.dot(c_rows, entering[:, cols], preferred_element_type=F32)
            z = z_ref[rows, cols].astype(F32)
            value = (acc_ref[rows, cols] + term * spread(grown, pair, mask)) * (
                z * lax.logistic(z)
            )
            gated[:, cols] = value
            squares = squares + value * value
        mean = jnp.sum(squares, axis=1, keepdims=True) * (1.0 / inner)
        scale = lax.rsqrt(mean + EPS)
        for col in range(0, inner, 128):
            cols = slice(col, col + 128)
            out_ref[rows, cols] = (gated[:, cols] * scale * gain_ref[:, cols].astype(F32)).astype(BF16)


def product_kernel(plan, first, sel_ref, *refs):
    count = len(plan)
    a_refs = refs[0:4]
    w_refs = refs[4 : 4 + count]
    at = 4 + count
    if not first:
        acc_in = refs[at]
        at += 1
    out_ref, a_buf, w_buf, acc, sem = refs[at : at + 5]

    def a_copy(j, which):
        return pltpu.make_async_copy(a_refs[which], a_buf.at[j], sem.at[0, j])

    def w_copy(i, line):
        lo = plan[i][1 + line]
        return pltpu.make_async_copy(
            w_refs[i], w_buf.at[plan[i][0], lo : lo + w_refs[i].shape[0], :], sem.at[1, i]
        )

    blocks = a_buf.shape[0]
    for j in range(blocks):

        @pl.when(sel_ref[j, 0] == 1)
        def _():
            for which in range(4):

                @pl.when(sel_ref[j, 1] == which)
                def _():
                    a_copy(j, which).start()

            for line in range(2):

                @pl.when(sel_ref[j, 2] == line)
                def _():
                    for i in range(count):
                        if plan[i][0] == j:
                            w_copy(i, line).start()

    if first:
        acc[...] = jnp.zeros_like(acc)
    else:
        keep = pltpu.make_async_copy(acc_in, acc, sem.at[0, 7])
        keep.start()
        keep.wait()
    tile = 256
    for j in range(blocks):

        @pl.when(sel_ref[j, 0] == 1)
        def _():
            a_copy(j, 0).wait()
            for i in range(count):
                if plan[i][0] == j:
                    w_copy(i, 0).wait()

            @pl.loop(0, acc.shape[1] // tile)
            def _(n):
                cols = pl.ds(pl.multiple_of(n * tile, tile), tile)
                acc[:, cols] += jnp.dot(
                    a_buf[j], w_buf[j, :, cols], preferred_element_type=F32
                )

    out_ref[...] = acc[...].astype(out_ref.dtype)


def product(sel, normed, pieces, plan, acc, last):
    blocks = 1 + max(entry[0] for entry in plan)
    rows, depth = normed[0].shape
    cols = pieces[0].shape[1]
    out = jax.ShapeDtypeStruct((rows, cols), BF16 if last else F32)
    operands = [sel, *normed, *pieces] + ([] if acc is None else [acc])
    return pl.pallas_call(
        functools.partial(product_kernel, plan, acc is None),
        out_shape=out,
        in_specs=[SMEM] + [ANY] * (len(operands) - 1),
        out_specs=VMEM,
        scratch_shapes=[
            pltpu.VMEM((blocks, rows, depth), BF16),
            pltpu.VMEM((blocks, depth, cols), BF16),
            pltpu.VMEM((rows, cols), F32),
            pltpu.SemaphoreType.DMA((2, 8)),
        ],
        compiler_params=params(),
        cost_estimate=pl.CostEstimate(
            flops=2 * rows * depth * cols * blocks, bytes_accessed=8 * rows * cols, transcendentals=0
        ),
    )(*operands)


def conv_states(x_in, b_in, c_in, halo, dt_in, taps, dt_bias, a_log):
    length, inner = x_in.shape
    heads = dt_in.shape[1]
    width = inner + 2 * STATE
    return pl.pallas_call(
        conv_states_kernel,
        out_shape=(
            jax.ShapeDtypeStruct((length, width), BF16),
            jax.ShapeDtypeStruct((length, heads), F32),
            jax.ShapeDtypeStruct((length, heads), F32),
            jax.ShapeDtypeStruct((STATE, inner), BF16),
            jax.ShapeDtypeStruct((STATE + 16, inner), BF16),
        ),
        in_specs=[VMEM] * 8,
        out_specs=(VMEM,) * 5,
        scratch_shapes=[pltpu.VMEM((length + 8, width), F32)],
        compiler_params=params(),
        cost_estimate=pl.CostEstimate(flops=10**8, bytes_accessed=10**7, transcendentals=10**6),
    )(x_in, b_in, c_in, halo, dt_in, taps, dt_bias, a_log)


def diagonal(xbc, cum, lstep, first, d_skip):
    length = xbc.shape[0]
    inner = first.shape[1]
    return pl.pallas_call(
        diagonal_kernel,
        out_shape=jax.ShapeDtypeStruct((length, inner), F32),
        in_specs=[VMEM] * 4 + [SMEM],
        out_specs=VMEM,
        compiler_params=params(),
        cost_estimate=pl.CostEstimate(flops=10**9, bytes_accessed=10**7, transcendentals=10**6),
    )(xbc, cum, lstep, first, d_skip)


def finish(acc, xbc, cum, z_in, near, far, gain):
    length, inner = acc.shape
    return pl.pallas_call(
        finish_kernel,
        out_shape=jax.ShapeDtypeStruct((length, inner), BF16),
        in_specs=[VMEM] * 7,
        out_specs=VMEM,
        scratch_shapes=[pltpu.VMEM((128, inner), F32)],
        compiler_params=params(),
        cost_estimate=pl.CostEstimate(flops=10**9, bytes_accessed=10**7, transcendentals=10**6),
    )(acc, xbc, cum, z_in, near, far, gain)


def decay_of(msg):
    return msg[STATE : STATE + 1].astype(F32) + msg[STATE + 8 : STATE + 9].astype(F32)


def joined(earlier, later):
    decay = decay_of(later)
    state = later[:STATE].astype(F32) + decay * earlier[:STATE].astype(F32)
    both = decay_of(earlier) * decay
    high = both.astype(BF16)
    low = (both - high.astype(F32)).astype(BF16)
    wide = (8, state.shape[1])
    return jnp.concatenate(
        [state.astype(BF16), jnp.broadcast_to(high, wide), jnp.broadcast_to(low, wide)], 0
    )


def hop(block, distance):
    count = lax.axis_size("ctx")
    return lax.ppermute(block, "ctx", [(i, i + distance) for i in range(count - distance)])


def before(msg):
    count = lax.axis_size("ctx")
    mine = lax.axis_index("ctx")
    near = hop(msg, 1)
    reach = 1
    run = msg
    prior = near
    far = None
    while reach < count:
        if reach == 1:
            run = jnp.where(mine > 0, joined(near, msg), msg)
        reach *= 2
        if reach >= count:
            break
        came = hop(run, reach)
        if 2 * reach >= count:
            far = came[:STATE]
            break
        prior = joined(came, prior)
        run = jnp.where(mine >= reach, joined(came, run), run)
    if far is None:
        far = jnp.zeros_like(near[:STATE])
    return prior, far


def swap_y(block, places, count):
    route = [(y * count + z, (1 - y) * count + z) for y in range(2) for z in places]
    return lax.ppermute(block, ("groups", "ctx"), route)


def gather_weight(out_weight):
    count = 4
    rows = out_weight.shape[0]
    half = rows // 2
    part = (rows * 5 // 16) // 16 * 16
    side = lax.axis_index("groups")
    mine = lax.dynamic_slice_in_dim(out_weight, side * half, half, 0)
    mine_far = lax.dynamic_slice_in_dim(out_weight, side * part, part, 0)
    rest_far = out_weight[2 * part :]

    def line(block, sources, distance):
        return lax.ppermute(block, "ctx", [(i, i + distance) for i in sources])

    r1 = line(mine, (0, 1, 2), 1)
    l1 = line(mine, (1, 2, 3), -1)
    r2 = line(r1, (1, 2), 1)
    l2 = line(l1, (1, 2), -1)
    yr1 = swap_y(r1, (1, 2, 3), count)
    yl1 = swap_y(l1, (0, 1, 2), count)
    ends = [(0, 3), (3, 0)]
    da = lax.ppermute(mine_far, "ctx", ends)
    db = lax.ppermute(rest_far, "ctx", ends)
    yr2 = swap_y(r2, (2, 3), count)
    yl2 = swap_y(l2, (0, 1), count)
    yda = swap_y(da, (0, 3), count)
    return r1, yr1, l1, yl1, r2, yr2, l2, yl2, da, yda, db, half, part


def fast_shards(
    x_in, z_in, b_in, c_in, dt_in, conv_x, conv_bc, dt_bias, a_log, d_skip, norm_gain, out_weight
):
    gathered = gather_weight(out_weight)
    normed = mixer(
        x_in, z_in, b_in, c_in, dt_in, conv_x, conv_bc, dt_bias, a_log, d_skip, norm_gain
    )
    over = lax.ppermute(normed, "tp", [(0, 2), (2, 0), (1, 3), (3, 1)])
    core = [(0, 1), (1, 0), (2, 3), (3, 2)]
    mate = lax.ppermute(normed, "tp", core)
    over_mate = lax.ppermute(over, "tp", core)
    normed_by_xor = [normed, mate, over, over_mate]
    r1, yr1, l1, yl1, r2, yr2, l2, yl2, da, yda, db, half, part = gathered
    mine = lax.axis_index("ctx")
    tp = lax.axis_index("tp")
    side = lax.axis_index("groups")

    def row(source, valid):
        source = jnp.clip(source, 0, 3)
        return [valid.astype(jnp.int32), jnp.bitwise_xor(source, tp), side]

    def table(*entries):
        return jnp.array([v for entry in entries for v in entry], jnp.int32).reshape(len(entries), 3)

    yes = mine >= 0
    sel1 = table(row(mine, yes), row(mine - 1, mine > 0), row(mine + 1, mine < 3))
    sel2 = table(row(mine - 2, mine > 1), row(mine + 2, mine < 2))
    sel3 = table(row(3 - mine, (mine == 0) | (mine == 3)))
    total = product(
        sel1, normed_by_xor, [out_weight, r1, yr1, l1, yl1],
        ((0, 0, 0), (1, 0, half), (1, half, 0), (2, 0, half), (2, half, 0)),
        None, False,
    )
    total = product(
        sel2, normed_by_xor, [r2, yr2, l2, yl2],
        ((0, 0, half), (0, half, 0), (1, 0, half), (1, half, 0)),
        total, False,
    )
    return product(
        sel3, normed_by_xor, [da, yda, db],
        ((0, 0, part), (0, part, 0), (0, 2 * part, 2 * part)),
        total, True,
    )


def mixer(x_in, z_in, b_in, c_in, dt_in, conv_x, conv_bc, dt_bias, a_log, d_skip, norm_gain):
    tail = x_in.shape[0] - 8
    halo = hop(jnp.concatenate([x_in[tail:], b_in[tail:], c_in[tail:]], 1), 1)
    taps = jnp.concatenate([conv_x, conv_bc[0], conv_bc[1]], 1).astype(F32)
    xbc, cum, lstep, first, msg = conv_states(
        x_in, b_in, c_in, halo, dt_in, taps, dt_bias[None], a_log[None]
    )
    near, far = before(msg)
    acc = diagonal(xbc, cum, lstep, first, d_skip)
    return finish(acc, xbc, cum, z_in, near, far, norm_gain[None])


def plain_shards(*args):
    out_weight = args[-1]
    weight = lax.all_gather(out_weight, "ctx", axis=0, tiled=True)
    normed = mixer(*args[:-1])
    gathered = lax.all_gather(normed, "tp", axis=1, tiled=True)
    return jnp.dot(gathered, weight, preferred_element_type=F32).astype(BF16)


def solution(mesh):
    sizes = dict(mesh.shape)
    fast = sizes["groups"] == 2 and sizes["ctx"] == 4 and sizes["tp"] == 4
    return jax.shard_map(
        fast_shards if fast else plain_shards,
        mesh=mesh,
        in_specs=(
            P(("groups", "ctx"), "tp"),
            P(("groups", "ctx"), "tp"),
            P(("groups", "ctx"), "tp"),
            P(("groups", "ctx"), "tp"),
            P(("groups", "ctx"), "tp"),
            P(None, "tp"),
            P(None, None, "tp"),
            P("tp"),
            P("tp"),
            P("tp"),
            P("tp"),
            P("ctx", "tp"),
        ),
        out_specs=P(("groups", "ctx"), "tp"),
        check_vma=False,
    )
```

```python
import functools
import jax
import jax.numpy as jnp
from jax import lax
from jax.experimental import pallas as pl
from jax.experimental.pallas import tpu as pltpu
from jax.sharding import PartitionSpec as P


STATE = 128
SPAN = 256
HALF = 128
EPS = 1e-05
FAR_ROWS = 320
LOG2E = 1.4426950408889634
F32 = jnp.float32
BF16 = jnp.bfloat16
HI = lax.Precision.HIGHEST
VMEM = pl.BlockSpec(memory_space=pltpu.VMEM)
SMEM = pl.BlockSpec(memory_space=pltpu.SMEM)
ANY = pl.BlockSpec(memory_space=pl.ANY)
HBM = pl.BlockSpec(memory_space=pltpu.HBM)


def params(mib):
    return pltpu.CompilerParams(vmem_limit_bytes=mib * 1024 * 1024)


def pair_lanes(rows, left):
    return lax.broadcasted_iota(jnp.int32, (rows, 2 * left), 1) < left


def spread(table, pair, mask):
    rows, lanes = mask.shape
    first = jnp.broadcast_to(table[:, 2 * pair : 2 * pair + 1], (rows, lanes))
    second = jnp.broadcast_to(table[:, 2 * pair + 1 : 2 * pair + 2], (rows, lanes))
    return jnp.where(mask, first, second)


def load(pairs, sem):
    copies = [
        pltpu.make_async_copy(source, target, sem.at[i]) for i, (source, target) in enumerate(pairs)
    ]
    for copy in copies:
        copy.start()
    return copies


def prepare_kernel(side_ref, x_ref, b_ref, c_ref, w_ref, halo_ref, head_ref, rear_ref, w_buf, sem):
    length, inner = x_ref.shape
    part, rest = head_ref.shape[0], rear_ref.shape[0]
    half = part + rest
    tail = pl.ds(length - 8, 8)
    own = pl.multiple_of(side_ref[0] * half, 16)
    cuts = ((0, part // 2), (part // 2, part // 2), (part, rest))
    ins = load(
        [
            (x_ref.at[tail], halo_ref.at[:, 0:inner]),
            (b_ref.at[tail], halo_ref.at[:, inner : inner + STATE]),
            (c_ref.at[tail], halo_ref.at[:, inner + STATE : inner + 2 * STATE]),
        ]
        + [(w_ref.at[pl.ds(own + at, rows)], w_buf.at[pl.ds(at, rows)]) for at, rows in cuts],
        sem,
    )
    outs = []
    for i, (at, rows) in enumerate(cuts):
        target = head_ref.at[pl.ds(at, rows)] if at < part else rear_ref
        outs.append(pltpu.make_async_copy(w_buf.at[pl.ds(at, rows)], target, sem.at[6 + i]))
        ins[3 + i].wait()
        outs[i].start()
    for i in range(3):
        ins[i].wait()
    for out in outs:
        out.wait()


def pick_kernel(count, place_ref, *refs):
    lower, upper, out_ref, buf, sem = refs[:count], refs[count : 2 * count], *refs[2 * count :]
    high = place_ref[0] * 2 >= place_ref[3]
    cuts = []
    at = 0
    for ref in lower:
        step = ref.shape[0] // 2
        for i in range(2):
            cuts.append((len(cuts) // 2, i * step, at, step))
            at += step
    for wanted, refs_here in ((high, lower), (jnp.logical_not(high), upper)):

        @pl.when(wanted)
        def _():
            for i, (piece, begin, at, rows) in enumerate(cuts):
                pltpu.make_async_copy(
                    refs_here[piece].at[pl.ds(begin, rows)], buf.at[pl.ds(at, rows)], sem.at[0, i]
                ).start()

    outs = []
    for i, (piece, begin, at, rows) in enumerate(cuts):
        pltpu.make_async_copy(
            lower[piece].at[pl.ds(begin, rows)], buf.at[pl.ds(at, rows)], sem.at[0, i]
        ).wait()
        outs.append(
            pltpu.make_async_copy(buf.at[pl.ds(at, rows)], out_ref.at[pl.ds(at, rows)], sem.at[1, i])
        )
        outs[i].start()
    for out in outs:
        out.wait()


def more_kernel(side_ref, w_ref, other_ref, rest_ref, w_buf, sem):
    half = other_ref.shape[0]
    rest = rest_ref.shape[0] // 2
    own = pl.multiple_of(side_ref[0] * half, 16)
    far = pl.multiple_of(half - own, 16)
    ins = load(
        [
            (w_ref.at[pl.ds(far, half)], w_buf.at[pl.ds(0, half)]),
            (w_ref.at[pl.ds(half - rest, rest)], w_buf.at[pl.ds(half, rest)]),
            (w_ref.at[pl.ds(2 * half - rest, rest)], w_buf.at[pl.ds(half + rest, rest)]),
        ],
        sem,
    )
    outs = [
        pltpu.make_async_copy(w_buf.at[pl.ds(0, half)], other_ref, sem.at[3]),
        pltpu.make_async_copy(
            w_buf.at[pl.ds(half, rest)], rest_ref.at[pl.ds(0, rest)], sem.at[4]
        ),
        pltpu.make_async_copy(
            w_buf.at[pl.ds(half + rest, rest)], rest_ref.at[pl.ds(rest, rest)], sem.at[5]
        ),
    ]
    for i in range(3):
        ins[i].wait()
        outs[i].start()
    for out in outs:
        out.wait()


def column(row):
    count = row.shape[1]
    same = lax.broadcasted_iota(jnp.int32, (count, count), 0) == lax.broadcasted_iota(
        jnp.int32, (count, count), 1
    )
    wide = jnp.broadcast_to(row, (count, count))
    return jnp.sum(jnp.where(same, wide, 0.0), axis=1, keepdims=True)


def conv_states_kernel(
    halo_ref, x_ref, b_ref, c_ref, dt_ref, convx_ref, convbc_ref, bias_ref, alog_ref,
    xbc_ref, cum_ref, back_ref, first_ref, msg_ref, ext,
):
    length, inner = x_ref.shape
    heads = dt_ref.shape[0]
    spans = length // SPAN
    width = ext.shape[1]
    chunk = 128
    value = dt_ref[...].astype(F32) + column(bias_ref[...])
    step = jnp.maximum(value, 0.0) + jnp.log1p(jnp.exp(-jnp.abs(value)))
    log_decay = step * (-jnp.exp(column(alog_ref[...])) * LOG2E)
    log_step = jnp.log2(step)
    rows_i = lax.broadcasted_iota(jnp.int32, (SPAN, SPAN), 0)
    cols_i = lax.broadcasted_iota(jnp.int32, (SPAN, SPAN), 1)
    lower = (rows_i >= cols_i).astype(F32)
    upper = (rows_i <= cols_i).astype(F32)
    eye = (rows_i == cols_i).astype(F32)
    turned = (((1,), (1,)), ((), ()))
    cums, ends = [], []
    for k in range(spans):
        rows = slice(k * SPAN, (k + 1) * SPAN)
        across = jnp.dot(log_decay[:, rows], upper, precision=HI, preferred_element_type=F32)
        back_ref[:, rows] = across - log_step[:, rows]
        cum = lax.dot_general(
            lower, log_decay[:, rows], turned, precision=HI, preferred_element_type=F32
        )
        cum_ref[rows, :] = cum
        own = lax.dot_general(
            eye, log_step[:, rows], turned, precision=HI, preferred_element_type=F32
        )
        last = cum[SPAN - 1 : SPAN]
        cums.append(last)
        ends.append(jnp.exp2(last - cum + own))
    total_log = cums[0]
    for k in range(1, spans):
        total_log = total_log + cums[k]
    ext[0:8, :] = halo_ref[...].astype(F32)
    ext[8:, inner : inner + STATE] = b_ref[...].astype(F32)
    ext[8:, inner + STATE :] = c_ref[...].astype(F32)
    ext[8:, 0:inner] = x_ref[...].astype(F32)
    taps_count = convx_ref.shape[0]
    for col in range(0, width, 128):
        if col < inner:
            taps = convx_ref[:, col : col + 128].astype(F32)
        else:
            taps = convbc_ref[(col - inner) // STATE].astype(F32)
        for row in range(0, length, chunk):
            total = jnp.zeros((chunk, 128), F32)
            for k in range(taps_count):
                start = 8 - (taps_count - 1) + k + row
                total = total + ext[start : start + chunk, col : col + 128] * taps[k : k + 1]
            xbc_ref[row : row + chunk, col : col + 128] = (
                total * lax.logistic(total)
            ).astype(BF16)
    head_dim = inner // heads
    mask = pair_lanes(SPAN, head_dim)
    row_mask = pair_lanes(8, head_dim)
    for pair in range(heads // 2):
        cols = slice(pair * 128, (pair + 1) * 128)
        state = None
        for k in range(spans):
            rows = slice(k * SPAN, (k + 1) * SPAN)
            weighted = (
                xbc_ref[rows, cols].astype(F32) * spread(ends[k], pair, mask)
            ).astype(BF16)
            local = lax.dot_general(
                xbc_ref[rows, inner : inner + STATE], weighted,
                (((0,), (0,)), ((), ())), preferred_element_type=F32,
            )
            if state is None:
                state = local
                first_ref[:, cols] = local.astype(BF16)
            else:
                decay = spread(jnp.broadcast_to(jnp.exp2(cums[k]), (8, heads)), pair, row_mask)
                state = decay[0:1] * state + local
        msg_ref[0:STATE, cols] = state.astype(BF16)
        gone = spread(jnp.broadcast_to(jnp.exp2(total_log), (8, heads)), pair, row_mask)
        high = gone.astype(BF16)
        low = (gone - high.astype(F32)).astype(BF16)
        msg_ref[STATE : STATE + 8, cols] = high
        msg_ref[STATE + 8 : STATE + 16, cols] = low


def diagonal_kernel(xbc_ref, cum_ref, back_ref, first_ref, skip_ref, acc_ref):
    length, inner = acc_ref.shape
    heads = cum_ref.shape[1]
    spans = length // SPAN
    head_dim = inner // heads
    mask = pair_lanes(SPAN, head_dim)
    half_mask = pair_lanes(HALF, head_dim)
    rows_i = lax.broadcasted_iota(jnp.int32, (SPAN, SPAN), 0)
    cols_i = lax.broadcasted_iota(jnp.int32, (SPAN, SPAN), 1)
    for k in range(spans):
        rows = slice(k * SPAN, (k + 1) * SPAN)
        cum = cum_ref[rows, :]
        back = back_ref[:, rows]
        b_span = xbc_ref[rows, inner : inner + STATE]
        c_span = xbc_ref[rows, inner + STATE :]
        scores = lax.dot_general(
            c_span, b_span, (((1,), (1,)), ((), ())), preferred_element_type=F32
        )
        scores = jnp.where(rows_i >= cols_i, scores, 0.0)
        if k:
            grown = jnp.exp2(cum)
        for pair in range(heads // 2):
            cols = slice(pair * 128, (pair + 1) * 128)
            x_pair = xbc_ref[rows, cols]
            tops, lows = [], []
            for h in (2 * pair, 2 * pair + 1):
                later = jnp.broadcast_to(cum[:, h : h + 1], (SPAN, HALF))
                row0 = back[h : h + 1, 0:HALF]
                row1 = back[h : h + 1, HALF:]
                m00 = scores[0:HALF, 0:HALF] * jnp.exp2(jnp.minimum(later[0:HALF] - row0, 100.0))
                m10 = scores[HALF:, 0:HALF] * jnp.exp2(later[HALF:] - row0)
                m11 = scores[HALF:, HALF:] * jnp.exp2(jnp.minimum(later[HALF:] - row1, 100.0))
                tops.append(jnp.dot(m00.astype(BF16), x_pair[0:HALF], preferred_element_type=F32))
                lows.append(
                    jnp.dot(
                        jnp.concatenate([m10.astype(BF16), m11.astype(BF16)], axis=1),
                        x_pair, preferred_element_type=F32,
                    )
                )
            top = jnp.where(half_mask, tops[0], tops[1])
            low = jnp.where(half_mask, lows[0], lows[1])
            skip = jnp.where(half_mask, skip_ref[2 * pair], skip_ref[2 * pair + 1])
            x_f = x_pair.astype(F32)
            top = top + skip * x_f[0:HALF]
            low = low + skip * x_f[HALF:]
            if k:
                inner_state = jnp.dot(c_span, first_ref[:, cols], preferred_element_type=F32)
                term = inner_state * spread(grown, pair, mask)
                top = top + term[0:HALF]
                low = low + term[HALF:]
            acc_ref[k * SPAN : k * SPAN + HALF, cols] = top
            acc_ref[k * SPAN + HALF : (k + 1) * SPAN, cols] = low


def finish_kernel(acc_ref, xbc_ref, cum_ref, z_hbm, near_ref, far_ref, gain_ref, out_ref, gated, z_ref, sem):
    length, inner = acc_ref.shape
    z_copy = load([(z_hbm, z_ref)], sem)[0]
    heads = cum_ref.shape[1]
    head_dim = inner // heads
    chunk = 128
    mask = pair_lanes(chunk, head_dim)
    decay = near_ref[STATE : STATE + 1, :].astype(F32) + near_ref[STATE + 8 : STATE + 9, :].astype(F32)
    entering = (
        near_ref[0:STATE, :].astype(F32) + decay * far_ref[...].astype(F32)
    ).astype(BF16)
    offset = jnp.zeros((1, heads), F32)
    z_copy.wait()
    for row in range(0, length, chunk):
        rows = slice(row, row + chunk)
        if row and row % SPAN == 0:
            offset = offset + cum_ref[row - 1 : row, :]
        grown = jnp.exp2(cum_ref[rows, :] + offset)
        c_rows = xbc_ref[rows, inner + STATE :]
        squares = jnp.zeros((chunk, 128), F32)
        for pair in range(heads // 2):
            cols = slice(pair * 128, (pair + 1) * 128)
            term = jnp.dot(c_rows, entering[:, cols], preferred_element_type=F32)
            z = z_ref[rows, cols].astype(F32)
            value = (acc_ref[rows, cols] + term * spread(grown, pair, mask)) * (
                z * lax.logistic(z)
            )
            gated[:, cols] = value
            squares = squares + value * value
        mean = jnp.sum(squares, axis=1, keepdims=True) * (1.0 / inner)
        scale = lax.rsqrt(mean + EPS)
        for col in range(0, inner, 128):
            cols = slice(col, col + 128)
            out_ref[rows, cols] = (gated[:, cols] * scale * gain_ref[:, cols].astype(F32)).astype(BF16)


def product_kernel(plan, first, place_ref, *refs):
    count = 1 + max(piece[0] for _, pieces in plan for piece in pieces)
    a_refs = refs[0:4]
    w_refs = refs[4 : 4 + count]
    at = 4 + count
    acc_in = None
    if not first:
        acc_in = refs[at]
        at += 1
    out_ref, a_buf, w_buf, acc, out_buf, sem = refs[at : at + 6]
    mine, tp, side = place_ref[0], place_ref[1], place_ref[2]
    last = place_ref[3] - 1
    tiles, _, tile = acc.shape
    blocks = len(plan)

    sources, valids = [], []
    for offset, _ in plan:
        if offset is None:
            source = last - mine
            valid = (mine == 0) | (mine == last)
        else:
            source = mine + offset
            valid = (source >= 0) & (source <= last)
        sources.append(source)
        valids.append(valid)

    numbered = []
    for j, (_, pieces) in enumerate(plan):
        for piece in pieces:
            numbered.append((j, piece))

    def a_copy(j, which):
        return pltpu.make_async_copy(a_refs[which], a_buf.at[j], sem.at[0, j])

    def w_copy(i, line, n):
        j, (array, begin, rows, *places, _) = numbered[i]
        cols = pl.ds(n * tile, tile)
        return pltpu.make_async_copy(
            w_refs[array].at[pl.ds(begin, rows), cols],
            w_buf.at[j, pl.ds(places[line], rows), cols],
            sem.at[1 + n, i],
        )

    def here(i):
        _, piece = numbered[i]
        found = mine == piece[-1][0]
        for place in piece[-1][1:]:
            found = found | (mine == place)
        return found

    def acc_copy(n):
        return pltpu.make_async_copy(acc_in.at[n], acc.at[n], sem.at[0, 4 + n])

    def out_copy(n):
        if out_buf is None:
            return pltpu.make_async_copy(acc.at[n], out_ref.at[n], sem.at[5, n])
        return pltpu.make_async_copy(
            out_buf.at[:, pl.ds(n * tile, tile)], out_ref.at[:, pl.ds(n * tile, tile)], sem.at[5, n]
        )

    for j in range(blocks):

        @pl.when(valids[j])
        def _():
            relation = jnp.bitwise_xor(sources[j], tp)
            for which in range(4):

                @pl.when(relation == which)
                def _():
                    a_copy(j, which).start()

    for i in range(len(numbered)):
        for line in range(2):

            @pl.when(here(i) & (side == line))
            def _():
                for n in range(tiles):
                    w_copy(i, line, n).start()

    if not first:
        for n in range(tiles):
            acc_copy(n).start()
    for j in range(blocks):

        @pl.when(valids[j])
        def _():
            a_copy(j, 0).wait()

    for n in range(tiles):
        if first:
            acc[n] = jnp.zeros(acc.shape[1:], F32)
        else:
            acc_copy(n).wait()
        for i in range(len(numbered)):

            @pl.when(here(i))
            def _():
                w_copy(i, 0, n).wait()

        for j in range(blocks):

            @pl.when(valids[j])
            def _():
                acc[n] += jnp.dot(
                    a_buf[j], w_buf[j, :, n * tile : (n + 1) * tile], preferred_element_type=F32
                )

        if out_buf is not None:
            out_buf[:, n * tile : (n + 1) * tile] = acc[n].astype(out_buf.dtype)
        out_copy(n).start()
    for n in range(tiles):
        out_copy(n).wait()


def plain_kernel(plan, first, final, place_ref, *refs):
    if final:
        return product_kernel(plan, first, place_ref, *refs)
    *front, sem = refs
    return product_kernel(plan, first, place_ref, *front, None, sem)


def product(place, normed, pieces, plan, acc, final):
    rows, depth = normed[0].shape
    cols = pieces[0].shape[1]
    tile = 256
    tiles = cols // tile
    if final:
        out = jax.ShapeDtypeStruct((rows, cols), BF16)
    else:
        out = jax.ShapeDtypeStruct((tiles, rows, tile), F32)
    operands = [place, *normed, *pieces] + ([] if acc is None else [acc])
    blocks = len(plan)
    scratch = [
        pltpu.VMEM((blocks, rows, depth), BF16),
        pltpu.VMEM((blocks, depth, cols), BF16),
        pltpu.VMEM((tiles, rows, tile), F32),
    ]
    if final:
        scratch.append(pltpu.VMEM((rows, cols), BF16))
    scratch.append(pltpu.SemaphoreType.DMA((6, 10)))
    return pl.pallas_call(
        functools.partial(plain_kernel, plan, acc is None, final),
        out_shape=out,
        in_specs=[SMEM] + [ANY] * 4 + [HBM] * (len(operands) - 5),
        out_specs=ANY,
        scratch_shapes=scratch,
        compiler_params=params(24),
        cost_estimate=pl.CostEstimate(
            flops=2 * rows * depth * cols * blocks, bytes_accessed=8 * rows * cols, transcendentals=0
        ),
    )(*operands)


def in_hbm(array):
    return pltpu.with_memory_space_constraint(array, pltpu.HBM)


def prepare(side, x_in, b_in, c_in, out_weight, part):
    rows, cols = out_weight.shape
    half = rows // 2
    width = x_in.shape[1] + 2 * STATE
    return pl.pallas_call(
        prepare_kernel,
        out_shape=(
            jax.ShapeDtypeStruct((8, width), BF16),
            jax.ShapeDtypeStruct((part, cols), BF16),
            jax.ShapeDtypeStruct((half - part, cols), BF16),
        ),
        in_specs=[SMEM] + [HBM] * 4,
        out_specs=(VMEM, HBM, HBM),
        scratch_shapes=[pltpu.VMEM((half, cols), BF16), pltpu.SemaphoreType.DMA((9,))],
        compiler_params=params(8),
        cost_estimate=pl.CostEstimate(flops=10**5, bytes_accessed=6 * 10**6, transcendentals=0),
    )(side, in_hbm(x_in), in_hbm(b_in), in_hbm(c_in), in_hbm(out_weight))


def pick(place, lower, upper):
    rows = sum(piece.shape[0] for piece in lower)
    cols = lower[0].shape[1]
    return pl.pallas_call(
        functools.partial(pick_kernel, len(lower)),
        out_shape=jax.ShapeDtypeStruct((rows, cols), BF16),
        in_specs=[SMEM] + [ANY] * (2 * len(lower)),
        out_specs=HBM,
        scratch_shapes=[
            pltpu.VMEM((rows, cols), BF16),
            pltpu.SemaphoreType.DMA((2, 2 * len(lower))),
        ],
        compiler_params=params(16),
        cost_estimate=pl.CostEstimate(flops=10**5, bytes_accessed=3 * 10**6, transcendentals=0),
    )(place, *lower, *upper)


def prepare_more(side, out_weight, rest):
    rows, cols = out_weight.shape
    half = rows // 2
    return pl.pallas_call(
        more_kernel,
        out_shape=(
            jax.ShapeDtypeStruct((half, cols), BF16),
            jax.ShapeDtypeStruct((2 * rest, cols), BF16),
        ),
        in_specs=[SMEM, HBM],
        out_specs=(HBM, HBM),
        scratch_shapes=[
            pltpu.VMEM((half + 2 * rest, cols), BF16),
            pltpu.SemaphoreType.DMA((6,)),
        ],
        compiler_params=params(8),
        cost_estimate=pl.CostEstimate(flops=10**5, bytes_accessed=6 * 10**6, transcendentals=0),
    )(side, in_hbm(out_weight))


def conv_states(x_in, b_in, c_in, halo, dt_in, conv_x, conv_bc, dt_bias, a_log):
    length, inner = x_in.shape
    heads = dt_in.shape[1]
    width = inner + 2 * STATE
    return pl.pallas_call(
        conv_states_kernel,
        out_shape=(
            jax.ShapeDtypeStruct((length, width), BF16),
            jax.ShapeDtypeStruct((length, heads), F32),
            jax.ShapeDtypeStruct((heads, length), F32),
            jax.ShapeDtypeStruct((STATE, inner), BF16),
            jax.ShapeDtypeStruct((STATE + 16, inner), BF16),
        ),
        in_specs=[VMEM] * 9,
        out_specs=(VMEM,) * 5,
        scratch_shapes=[pltpu.VMEM((length + 8, width), F32)],
        compiler_params=params(16),
        cost_estimate=pl.CostEstimate(flops=10**8, bytes_accessed=10**7, transcendentals=10**6),
    )(halo, x_in, b_in, c_in, dt_in.T, conv_x, conv_bc, dt_bias[None], a_log[None])


def diagonal(xbc, cum, back, first, d_skip):
    length = xbc.shape[0]
    inner = first.shape[1]
    return pl.pallas_call(
        diagonal_kernel,
        out_shape=jax.ShapeDtypeStruct((length, inner), F32),
        in_specs=[VMEM] * 4 + [SMEM],
        out_specs=VMEM,
        compiler_params=params(16),
        cost_estimate=pl.CostEstimate(flops=10**9, bytes_accessed=10**7, transcendentals=10**6),
    )(xbc, cum, back, first, d_skip)


def finish(acc, xbc, cum, z_in, near, far, gain):
    length, inner = acc.shape
    return pl.pallas_call(
        finish_kernel,
        out_shape=jax.ShapeDtypeStruct((length, inner), BF16),
        in_specs=[VMEM] * 3 + [HBM] + [VMEM] * 3,
        out_specs=VMEM,
        scratch_shapes=[
            pltpu.VMEM((128, inner), F32),
            pltpu.VMEM((length, inner), BF16),
            pltpu.SemaphoreType.DMA((1,)),
        ],
        compiler_params=params(16),
        cost_estimate=pl.CostEstimate(flops=10**9, bytes_accessed=10**7, transcendentals=10**6),
    )(acc, xbc, cum, z_in, near, far, gain)


def decay_of(msg):
    return msg[STATE : STATE + 1].astype(F32) + msg[STATE + 8 : STATE + 9].astype(F32)


def joined(earlier, later):
    decay = decay_of(later)
    state = later[:STATE].astype(F32) + decay * earlier[:STATE].astype(F32)
    both = decay_of(earlier) * decay
    high = both.astype(BF16)
    low = (both - high.astype(F32)).astype(BF16)
    wide = (8, state.shape[1])
    return jnp.concatenate(
        [state.astype(BF16), jnp.broadcast_to(high, wide), jnp.broadcast_to(low, wide)], 0
    )


def hop(block, distance):
    count = lax.axis_size("ctx")
    return lax.ppermute(block, "ctx", [(i, i + distance) for i in range(count - distance)])


def extend_kernel(near_ref, msg_ref, out_ref):
    decay = msg_ref[STATE : STATE + 1].astype(F32) + msg_ref[STATE + 8 : STATE + 9].astype(F32)
    out_ref[...] = (
        msg_ref[0:STATE].astype(F32) + decay * near_ref[0:STATE].astype(F32)
    ).astype(BF16)


def extend(near, msg):
    return pl.pallas_call(
        extend_kernel,
        out_shape=jax.ShapeDtypeStruct((STATE, msg.shape[1]), BF16),
        in_specs=[VMEM] * 2,
        out_specs=VMEM,
        compiler_params=params(4),
        cost_estimate=pl.CostEstimate(flops=10**5, bytes_accessed=10**6, transcendentals=0),
    )(near, msg)


def before(msg):
    count = lax.axis_size("ctx")
    near = hop(msg, 1)
    if count <= 2:
        return near, jnp.zeros_like(near[:STATE])
    reach, run, prior = 2, msg, near
    if count > 4:
        run = joined(near, msg)
    while 2 * reach < count:
        came = hop(run, reach)
        prior = joined(came, prior)
        run = joined(came, run)
        reach *= 2
    run = extend(near, msg) if count <= 4 else run[:STATE]
    return prior, hop(run, reach)


def swap_y(block, places, count):
    route = [(y * count + z, (1 - y) * count + z) for y in range(2) for z in places]
    return lax.ppermute(block, ("groups", "ctx"), route)


def line(block, sources, distance):
    return lax.ppermute(block, "ctx", [(i, i + distance) for i in sources])


def across(block, route):
    return lax.ppermute(block, "tp", route)


def fast_shards(*args):
    return fast_layer(*args)


def fast_layer(
    x_in, z_in, b_in, c_in, dt_in, conv_x, conv_bc, dt_bias, a_log, d_skip, norm_gain, out_weight
):
    count = 4
    rows = out_weight.shape[0]
    half = rows // 2
    part = FAR_ROWS
    rest = half - part
    place = jnp.stack(
        [lax.axis_index("ctx"), lax.axis_index("tp"), lax.axis_index("groups"), jnp.int32(count)]
    ).astype(jnp.int32)
    side = lax.axis_index("groups")[None].astype(jnp.int32)
    rim, head, rear = prepare(side, x_in, b_in, c_in, out_weight, part)
    other, rest_far = prepare_more(side, out_weight, rest)
    halo = hop(rim, 1)
    r1a = line(head, (0, 1, 2), 1)
    l1a = line(head, (1, 2, 3), -1)
    r1b = line(rear, (0, 1, 2), 1)
    l1b = line(rear, (1, 2, 3), -1)
    full = lax.ppermute(other, "ctx", ((0, 1), (3, 2)))
    r2a = line(r1a, (1, 2), 1)
    l2a = line(l1a, (1, 2), -1)
    r2b = line(r1b, (1, 2), 1)
    l2b = line(l1b, (1, 2), -1)
    everywhere = (0, 1, 2, 3)
    y1 = swap_y(pick(place, [r1a, r1b], [l1a, l1b]), everywhere, count)
    head2 = pick(place, [r2a], [l2a])
    y2a = swap_y(head2, everywhere, count)
    y2b = swap_y(pick(place, [r2b], [l2b]), everywhere, count)
    far = lax.ppermute(head2, "ctx", ((2, 3), (1, 0)))
    y3 = swap_y(far, (0, 3), count)
    db = lax.ppermute(rest_far, "ctx", ((0, 3), (3, 0)))

    normed = mixer(
        halo, x_in, z_in, b_in, c_in, dt_in, conv_x, conv_bc, dt_bias, a_log, d_skip, norm_gain
    )
    over = across(normed, ((0, 2), (2, 0), (1, 3), (3, 1)))
    core = ((0, 1), (1, 0), (2, 3), (3, 2))
    mate = across(normed, core)
    over_mate = across(over, core)
    all_normed = [normed, mate, over, over_mate]
    own_weight = in_hbm(out_weight)
    total = product(
        place, all_normed, [own_weight, r1a, r1b, l1a, l1b, full, y1],
        (
            (0, ((0, 0, rows, 0, 0, (0, 1, 2, 3)),)),
            (-1, (
                (1, 0, part, 0, half, (1, 2, 3)),
                (2, 0, rest, part, half + part, (1, 2, 3)),
                (6, 0, half, half, 0, (2, 3)),
                (5, 0, half, half, 0, (1,)),
            )),
            (1, (
                (3, 0, part, 0, half, (0, 1, 2)),
                (4, 0, rest, part, half + part, (0, 1, 2)),
                (6, 0, half, half, 0, (0, 1)),
                (5, 0, half, half, 0, (2,)),
            )),
        ),
        None, False,
    )
    total = product(
        place, all_normed, [r2a, r2b, l2a, l2b, y2a, y2b],
        (
            (-2, (
                (0, 0, part, 0, half, (2, 3)),
                (1, 0, rest, part, half + part, (2, 3)),
                (4, 0, part, half, 0, (2, 3)),
                (5, 0, rest, half + part, part, (2, 3)),
            )),
            (2, (
                (2, 0, part, 0, half, (0, 1)),
                (3, 0, rest, part, half + part, (0, 1)),
                (4, 0, part, half, 0, (0, 1)),
                (5, 0, rest, half + part, part, (0, 1)),
            )),
        ),
        total, False,
    )
    return product(
        place, all_normed, [far, y3, db],
        (
            (None, (
                (0, 0, part, 0, half, (0, 3)),
                (1, 0, part, half, 0, (0, 3)),
                (2, 0, rest, part, part, (0, 3)),
                (2, rest, rest, half + part, half + part, (0, 3)),
            )),
        ),
        total, True,
    )


def mixer(halo, x_in, z_in, b_in, c_in, dt_in, conv_x, conv_bc, dt_bias, a_log, d_skip, norm_gain):
    xbc, cum, back, first, msg = conv_states(
        x_in, b_in, c_in, halo, dt_in, conv_x, conv_bc, dt_bias, a_log
    )
    near, far = before(msg)
    acc = diagonal(xbc, cum, back, first, d_skip)
    return finish(acc, xbc, cum, z_in, near, far, norm_gain[None])


def plain_shards(*args):
    out_weight = args[-1]
    weight = lax.all_gather(out_weight, "ctx", axis=0, tiled=True)
    x_in, _, b_in, c_in = args[:4]
    tail = x_in.shape[0] - 8
    halo = hop(jnp.concatenate([x_in[tail:], b_in[tail:], c_in[tail:]], 1), 1)
    normed = mixer(halo, *args[:-1])
    gathered = lax.all_gather(normed, "tp", axis=1, tiled=True)
    return jnp.dot(gathered, weight, preferred_element_type=F32).astype(BF16)


def solution(mesh):
    sizes = dict(mesh.shape)
    fast = sizes["groups"] == 2 and sizes["ctx"] == 4 and sizes["tp"] == 4
    return jax.shard_map(
        fast_shards if fast else plain_shards,
        mesh=mesh,
        in_specs=(
            P(("groups", "ctx"), "tp"),
            P(("groups", "ctx"), "tp"),
            P(("groups", "ctx"), "tp"),
            P(("groups", "ctx"), "tp"),
            P(("groups", "ctx"), "tp"),
            P(None, "tp"),
            P(None, None, "tp"),
            P("tp"),
            P("tp"),
            P("tp"),
            P("tp"),
            P("ctx", "tp"),
        ),
        out_specs=P(("groups", "ctx"), "tp"),
        check_vma=False,
    )
```

```python
import functools
import jax
import jax.numpy as jnp
from jax import lax
from jax.experimental import pallas as pl
from jax.experimental.pallas import tpu as pltpu
from jax.sharding import PartitionSpec as P


STATE = 128
SPAN = 256
HALF = 128
EPS = 1e-05
FAR_ROWS = 320
LOG2E = 1.4426950408889634
F32 = jnp.float32
BF16 = jnp.bfloat16
HI = lax.Precision.HIGHEST
VMEM = pl.BlockSpec(memory_space=pltpu.VMEM)
SMEM = pl.BlockSpec(memory_space=pltpu.SMEM)
ANY = pl.BlockSpec(memory_space=pl.ANY)
HBM = pl.BlockSpec(memory_space=pltpu.HBM)


def params(mib):
    return pltpu.CompilerParams(vmem_limit_bytes=mib * 1024 * 1024)


def pair_lanes(rows, left):
    return lax.broadcasted_iota(jnp.int32, (rows, 2 * left), 1) < left


def spread(table, pair, mask):
    rows, lanes = mask.shape
    first = jnp.broadcast_to(table[:, 2 * pair : 2 * pair + 1], (rows, lanes))
    second = jnp.broadcast_to(table[:, 2 * pair + 1 : 2 * pair + 2], (rows, lanes))
    return jnp.where(mask, first, second)


def load(pairs, sem):
    copies = [
        pltpu.make_async_copy(source, target, sem.at[i]) for i, (source, target) in enumerate(pairs)
    ]
    for copy in copies:
        copy.start()
    return copies


def prepare_kernel(side_ref, x_ref, b_ref, c_ref, w_ref, halo_ref, head_ref, rear_ref, w_buf, sem):
    length, inner = x_ref.shape
    part, rest = head_ref.shape[0], rear_ref.shape[0]
    half = part + rest
    tail = pl.ds(length - 8, 8)
    own = pl.multiple_of(side_ref[0] * half, 16)
    cuts = ((0, part // 2), (part // 2, part // 2), (part, rest))
    ins = load(
        [
            (x_ref.at[tail], halo_ref.at[:, 0:inner]),
            (b_ref.at[tail], halo_ref.at[:, inner : inner + STATE]),
            (c_ref.at[tail], halo_ref.at[:, inner + STATE : inner + 2 * STATE]),
        ]
        + [(w_ref.at[pl.ds(own + at, rows)], w_buf.at[pl.ds(at, rows)]) for at, rows in cuts],
        sem,
    )
    outs = []
    for i, (at, rows) in enumerate(cuts):
        target = head_ref.at[pl.ds(at, rows)] if at < part else rear_ref
        outs.append(pltpu.make_async_copy(w_buf.at[pl.ds(at, rows)], target, sem.at[6 + i]))
        ins[3 + i].wait()
        outs[i].start()
    for i in range(3):
        ins[i].wait()
    for out in outs:
        out.wait()


def pick_kernel(places, place_ref, *refs):
    *arrays, out_ref, buf, sem = refs
    step = buf.shape[0] // 2
    for array, mine in zip(arrays, places):
        found = place_ref[0] == mine[0]
        for other in mine[1:]:
            found = found | (place_ref[0] == other)

        @pl.when(found)
        def _():
            for i in range(2):
                rows = pl.ds(i * step, step)
                pltpu.make_async_copy(array.at[rows], buf.at[rows], sem.at[0, i]).start()

    outs = []
    for i in range(2):
        rows = pl.ds(i * step, step)
        pltpu.make_async_copy(arrays[0].at[rows], buf.at[rows], sem.at[0, i]).wait()
        outs.append(pltpu.make_async_copy(buf.at[rows], out_ref.at[rows], sem.at[1, i]))
        outs[i].start()
    for out in outs:
        out.wait()


def more_kernel(side_ref, w_ref, other_ref, rest_ref, w_buf, sem):
    half = other_ref.shape[0]
    rest = rest_ref.shape[0] // 2
    own = pl.multiple_of(side_ref[0] * half, 16)
    far = pl.multiple_of(half - own, 16)
    ins = load(
        [
            (w_ref.at[pl.ds(far, half)], w_buf.at[pl.ds(0, half)]),
            (w_ref.at[pl.ds(half - rest, rest)], w_buf.at[pl.ds(half, rest)]),
            (w_ref.at[pl.ds(2 * half - rest, rest)], w_buf.at[pl.ds(half + rest, rest)]),
        ],
        sem,
    )
    outs = [
        pltpu.make_async_copy(w_buf.at[pl.ds(0, half)], other_ref, sem.at[3]),
        pltpu.make_async_copy(
            w_buf.at[pl.ds(half, rest)], rest_ref.at[pl.ds(0, rest)], sem.at[4]
        ),
        pltpu.make_async_copy(
            w_buf.at[pl.ds(half + rest, rest)], rest_ref.at[pl.ds(rest, rest)], sem.at[5]
        ),
    ]
    for i in range(3):
        ins[i].wait()
        outs[i].start()
    for out in outs:
        out.wait()


def column(row):
    count = row.shape[1]
    same = lax.broadcasted_iota(jnp.int32, (count, count), 0) == lax.broadcasted_iota(
        jnp.int32, (count, count), 1
    )
    wide = jnp.broadcast_to(row, (count, count))
    return jnp.sum(jnp.where(same, wide, 0.0), axis=1, keepdims=True)


def conv_states_kernel(
    halo_ref, x_ref, b_ref, c_ref, dt_ref, convx_ref, convbc_ref, bias_ref, alog_ref,
    xbc_ref, cum_ref, back_ref, first_ref, state_ref, decay_ref, ext,
):
    length, inner = x_ref.shape
    heads = dt_ref.shape[0]
    spans = length // SPAN
    width = ext.shape[1]
    chunk = 128
    value = dt_ref[...].astype(F32) + column(bias_ref[...])
    step = jnp.maximum(value, 0.0) + jnp.log1p(jnp.exp(-jnp.abs(value)))
    log_decay = step * (-jnp.exp(column(alog_ref[...])) * LOG2E)
    log_step = jnp.log2(step)
    rows_i = lax.broadcasted_iota(jnp.int32, (SPAN, SPAN), 0)
    cols_i = lax.broadcasted_iota(jnp.int32, (SPAN, SPAN), 1)
    lower = (rows_i >= cols_i).astype(F32)
    upper = (rows_i <= cols_i).astype(F32)
    eye = (rows_i == cols_i).astype(F32)
    turned = (((1,), (1,)), ((), ()))
    cums, ends = [], []
    for k in range(spans):
        rows = slice(k * SPAN, (k + 1) * SPAN)
        across = jnp.dot(log_decay[:, rows], upper, precision=HI, preferred_element_type=F32)
        back_ref[:, rows] = across - log_step[:, rows]
        cum = lax.dot_general(
            lower, log_decay[:, rows], turned, precision=HI, preferred_element_type=F32
        )
        cum_ref[rows, :] = cum
        own = lax.dot_general(
            eye, log_step[:, rows], turned, precision=HI, preferred_element_type=F32
        )
        last = cum[SPAN - 1 : SPAN]
        cums.append(last)
        ends.append(jnp.exp2(last - cum + own))
    total_log = cums[0]
    for k in range(1, spans):
        total_log = total_log + cums[k]
    ext[0:8, :] = halo_ref[...].astype(F32)
    ext[8:, inner : inner + STATE] = b_ref[...].astype(F32)
    ext[8:, inner + STATE :] = c_ref[...].astype(F32)
    ext[8:, 0:inner] = x_ref[...].astype(F32)
    taps_count = convx_ref.shape[0]
    for col in range(0, width, 128):
        if col < inner:
            taps = convx_ref[:, col : col + 128].astype(F32)
        else:
            taps = convbc_ref[(col - inner) // STATE].astype(F32)
        for row in range(0, length, chunk):
            total = jnp.zeros((chunk, 128), F32)
            for k in range(taps_count):
                start = 8 - (taps_count - 1) + k + row
                total = total + ext[start : start + chunk, col : col + 128] * taps[k : k + 1]
            xbc_ref[row : row + chunk, col : col + 128] = (
                total * lax.logistic(total)
            ).astype(BF16)
    head_dim = inner // heads
    mask = pair_lanes(SPAN, head_dim)
    row_mask = pair_lanes(8, head_dim)
    for pair in range(heads // 2):
        cols = slice(pair * 128, (pair + 1) * 128)
        state = None
        for k in range(spans):
            rows = slice(k * SPAN, (k + 1) * SPAN)
            weighted = (
                xbc_ref[rows, cols].astype(F32) * spread(ends[k], pair, mask)
            ).astype(BF16)
            local = lax.dot_general(
                xbc_ref[rows, inner : inner + STATE], weighted,
                (((0,), (0,)), ((), ())), preferred_element_type=F32,
            )
            if state is None:
                state = local
                first_ref[:, cols] = local.astype(BF16)
            else:
                decay = spread(jnp.broadcast_to(jnp.exp2(cums[k]), (8, heads)), pair, row_mask)
                state = decay[0:1] * state + local
        state_ref[:, cols] = state.astype(BF16)
        gone = spread(jnp.broadcast_to(jnp.exp2(total_log), (8, heads)), pair, row_mask)
        high = gone.astype(BF16)
        low = (gone - high.astype(F32)).astype(BF16)
        decay_ref[0:8, cols] = high
        decay_ref[8:16, cols] = low


def diagonal_kernel(xbc_ref, cum_ref, back_ref, first_ref, skip_ref, acc_ref):
    length, inner = acc_ref.shape
    heads = cum_ref.shape[1]
    spans = length // SPAN
    head_dim = inner // heads
    mask = pair_lanes(SPAN, head_dim)
    half_mask = pair_lanes(HALF, head_dim)
    rows_i = lax.broadcasted_iota(jnp.int32, (SPAN, SPAN), 0)
    cols_i = lax.broadcasted_iota(jnp.int32, (SPAN, SPAN), 1)
    for k in range(spans):
        rows = slice(k * SPAN, (k + 1) * SPAN)
        cum = cum_ref[rows, :]
        back = back_ref[:, rows]
        b_span = xbc_ref[rows, inner : inner + STATE]
        c_span = xbc_ref[rows, inner + STATE :]
        scores = lax.dot_general(
            c_span, b_span, (((1,), (1,)), ((), ())), preferred_element_type=F32
        )
        scores = jnp.where(rows_i >= cols_i, scores, 0.0)
        if k:
            grown = jnp.exp2(cum)
        for pair in range(heads // 2):
            cols = slice(pair * 128, (pair + 1) * 128)
            x_pair = xbc_ref[rows, cols]
            tops, lows = [], []
            for h in (2 * pair, 2 * pair + 1):
                later = jnp.broadcast_to(cum[:, h : h + 1], (SPAN, HALF))
                row0 = back[h : h + 1, 0:HALF]
                row1 = back[h : h + 1, HALF:]
                m00 = scores[0:HALF, 0:HALF] * jnp.exp2(jnp.minimum(later[0:HALF] - row0, 100.0))
                m10 = scores[HALF:, 0:HALF] * jnp.exp2(later[HALF:] - row0)
                m11 = scores[HALF:, HALF:] * jnp.exp2(jnp.minimum(later[HALF:] - row1, 100.0))
                tops.append(jnp.dot(m00.astype(BF16), x_pair[0:HALF], preferred_element_type=F32))
                lows.append(
                    jnp.dot(
                        jnp.concatenate([m10.astype(BF16), m11.astype(BF16)], axis=1),
                        x_pair, preferred_element_type=F32,
                    )
                )
            top = jnp.where(half_mask, tops[0], tops[1])
            low = jnp.where(half_mask, lows[0], lows[1])
            skip = jnp.where(half_mask, skip_ref[2 * pair], skip_ref[2 * pair + 1])
            x_f = x_pair.astype(F32)
            top = top + skip * x_f[0:HALF]
            low = low + skip * x_f[HALF:]
            if k:
                inner_state = jnp.dot(c_span, first_ref[:, cols], preferred_element_type=F32)
                term = inner_state * spread(grown, pair, mask)
                top = top + term[0:HALF]
                low = low + term[HALF:]
            acc_ref[k * SPAN : k * SPAN + HALF, cols] = top
            acc_ref[k * SPAN + HALF : (k + 1) * SPAN, cols] = low


def finish_kernel(acc_ref, xbc_ref, cum_ref, z_hbm, gain_ref, *refs):
    *came, out_ref, gated, z_ref, sem = refs
    length, inner = acc_ref.shape
    z_copy = load([(z_hbm, z_ref)], sem)[0]
    heads = cum_ref.shape[1]
    head_dim = inner // heads
    chunk = 128
    mask = pair_lanes(chunk, head_dim)
    entering = came[0][...]
    for other in came[1:]:
        entering = entering + other[...]
    offset = jnp.zeros((1, heads), F32)
    z_copy.wait()
    for row in range(0, length, chunk):
        rows = slice(row, row + chunk)
        if row and row % SPAN == 0:
            offset = offset + cum_ref[row - 1 : row, :]
        grown = jnp.exp2(cum_ref[rows, :] + offset)
        c_rows = xbc_ref[rows, inner + STATE :]
        squares = jnp.zeros((chunk, 128), F32)
        for pair in range(heads // 2):
            cols = slice(pair * 128, (pair + 1) * 128)
            term = jnp.dot(c_rows, entering[:, cols], preferred_element_type=F32)
            z = z_ref[rows, cols].astype(F32)
            value = (acc_ref[rows, cols] + term * spread(grown, pair, mask)) * (
                z * lax.logistic(z)
            )
            gated[:, cols] = value
            squares = squares + value * value
        mean = jnp.sum(squares, axis=1, keepdims=True) * (1.0 / inner)
        scale = lax.rsqrt(mean + EPS)
        for col in range(0, inner, 128):
            cols = slice(col, col + 128)
            out_ref[rows, cols] = (gated[:, cols] * scale * gain_ref[:, cols].astype(F32)).astype(BF16)


def product_kernel(plan, first, place_ref, *refs):
    count = 1 + max(piece[0] for block in plan for piece in block[3])
    a_refs = refs[0:4]
    w_refs = refs[4 : 4 + count]
    at = 4 + count
    acc_in = None
    if not first:
        acc_in = refs[at]
        at += 1
    out_ref, a_buf, w_buf, acc, out_buf, sem = refs[at : at + 6]
    mine, tp, side = place_ref[0], place_ref[1], place_ref[2]
    last = place_ref[3] - 1
    tiles, _, tile = acc.shape
    slots = a_buf.shape[0]

    def among(places):
        found = mine == places[0]
        for place in places[1:]:
            found = found | (mine == place)
        return found

    has = [among(block[2]) for block in plan]
    covered = [
        sorted(place for block in plan if block[0] == slot for place in block[2])
        for slot in range(slots)
    ]

    def a_copy(slot, which):
        return pltpu.make_async_copy(a_refs[which], a_buf.at[slot], sem.at[0, slot])

    def w_copies(j, line, n):
        cols = pl.ds(n * tile, tile)
        return [
            pltpu.make_async_copy(
                w_refs[array].at[pl.ds(begin, rows), cols],
                w_buf.at[plan[j][0], pl.ds(places[line], rows), cols],
                sem.at[1 + n, 4 * plan[j][0] + i],
            )
            for i, (array, begin, rows, *places) in enumerate(plan[j][3])
        ]

    def acc_copy(n):
        return pltpu.make_async_copy(acc_in.at[n], acc.at[n], sem.at[0, 4 + n])

    def out_copy(n):
        if out_buf is None:
            return pltpu.make_async_copy(acc.at[n], out_ref.at[n], sem.at[5, n])
        return pltpu.make_async_copy(
            out_buf.at[:, pl.ds(n * tile, tile)], out_ref.at[:, pl.ds(n * tile, tile)], sem.at[5, n]
        )

    if not first:
        acc_copy(0).start()
    for j, (slot, offset, _, _) in enumerate(plan):
        source = last - mine if offset is None else mine + offset

        @pl.when(has[j])
        def _():
            relation = jnp.bitwise_xor(source, tp)
            for which in range(4):

                @pl.when(relation == which)
                def _():
                    a_copy(slot, which).start()

    for n in range(tiles):
        for j in range(len(plan)):
            for line in range(2):

                @pl.when(has[j] & (side == line))
                def _():
                    for copy in w_copies(j, line, n):
                        copy.start()

        if not first and n + 1 < tiles:
            acc_copy(n + 1).start()

    def add(slot, n):
        return jnp.dot(
            a_buf[slot], w_buf[slot, :, n * tile : (n + 1) * tile], preferred_element_type=F32
        )

    for slot in range(slots):

        @pl.when(among(covered[slot]))
        def _():
            a_copy(slot, 0).wait()

    for n in range(tiles):
        if not first:
            acc_copy(n).wait()
        for j in range(len(plan)):

            @pl.when(has[j])
            def _():
                for copy in w_copies(j, 0, n):
                    copy.wait()

        for slot in range(slots):
            if first and slot == 0:
                acc[n] = add(slot, n)
                continue

            @pl.when(among(covered[slot]))
            def _():
                acc[n] += add(slot, n)

        if out_buf is not None:
            out_buf[:, n * tile : (n + 1) * tile] = acc[n].astype(out_buf.dtype)
        out_copy(n).start()
    for n in range(tiles):
        out_copy(n).wait()


def plain_kernel(plan, first, final, place_ref, *refs):
    if final:
        return product_kernel(plan, first, place_ref, *refs)
    *front, sem = refs
    return product_kernel(plan, first, place_ref, *front, None, sem)


def product(place, normed, pieces, plan, acc, final):
    rows, depth = normed[0].shape
    cols = pieces[0].shape[1]
    tile = 256
    tiles = cols // tile
    if final:
        out = jax.ShapeDtypeStruct((rows, cols), BF16)
    else:
        out = jax.ShapeDtypeStruct((tiles, rows, tile), F32)
    operands = [place, *normed, *pieces] + ([] if acc is None else [acc])
    blocks = 1 + max(block[0] for block in plan)
    scratch = [
        pltpu.VMEM((blocks, rows, depth), BF16),
        pltpu.VMEM((blocks, depth, cols), BF16),
        pltpu.VMEM((tiles, rows, tile), F32),
    ]
    if final:
        scratch.append(pltpu.VMEM((rows, cols), BF16))
    scratch.append(pltpu.SemaphoreType.DMA((6, 8)))
    return pl.pallas_call(
        functools.partial(plain_kernel, plan, acc is None, final),
        out_shape=out,
        in_specs=[SMEM] + [ANY] * 4 + [HBM] * (len(operands) - 5),
        out_specs=ANY,
        scratch_shapes=scratch,
        compiler_params=params(24),
        cost_estimate=pl.CostEstimate(
            flops=2 * rows * depth * cols * blocks, bytes_accessed=8 * rows * cols, transcendentals=0
        ),
    )(*operands)


def in_hbm(array):
    return pltpu.with_memory_space_constraint(array, pltpu.HBM)


def prepare(side, x_in, b_in, c_in, out_weight, part):
    rows, cols = out_weight.shape
    half = rows // 2
    width = x_in.shape[1] + 2 * STATE
    return pl.pallas_call(
        prepare_kernel,
        out_shape=(
            jax.ShapeDtypeStruct((8, width), BF16),
            jax.ShapeDtypeStruct((part, cols), BF16),
            jax.ShapeDtypeStruct((half - part, cols), BF16),
        ),
        in_specs=[SMEM] + [HBM] * 4,
        out_specs=(VMEM, HBM, HBM),
        scratch_shapes=[pltpu.VMEM((half, cols), BF16), pltpu.SemaphoreType.DMA((9,))],
        compiler_params=params(8),
        cost_estimate=pl.CostEstimate(flops=10**5, bytes_accessed=6 * 10**6, transcendentals=0),
    )(side, in_hbm(x_in), in_hbm(b_in), in_hbm(c_in), in_hbm(out_weight))


def pick(place, *choices):
    arrays = [array for array, _ in choices]
    shape = arrays[0].shape
    return pl.pallas_call(
        functools.partial(pick_kernel, [places for _, places in choices]),
        out_shape=jax.ShapeDtypeStruct(shape, BF16),
        in_specs=[SMEM] + [ANY] * len(arrays),
        out_specs=HBM,
        scratch_shapes=[pltpu.VMEM(shape, BF16), pltpu.SemaphoreType.DMA((2, 2))],
        compiler_params=params(16),
        cost_estimate=pl.CostEstimate(flops=10**5, bytes_accessed=3 * 10**6, transcendentals=0),
    )(place, *arrays)


def prepare_more(side, out_weight, rest):
    rows, cols = out_weight.shape
    half = rows // 2
    return pl.pallas_call(
        more_kernel,
        out_shape=(
            jax.ShapeDtypeStruct((half, cols), BF16),
            jax.ShapeDtypeStruct((2 * rest, cols), BF16),
        ),
        in_specs=[SMEM, HBM],
        out_specs=(HBM, HBM),
        scratch_shapes=[
            pltpu.VMEM((half + 2 * rest, cols), BF16),
            pltpu.SemaphoreType.DMA((6,)),
        ],
        compiler_params=params(8),
        cost_estimate=pl.CostEstimate(flops=10**5, bytes_accessed=6 * 10**6, transcendentals=0),
    )(side, in_hbm(out_weight))


def conv_states(x_in, b_in, c_in, halo, dt_in, conv_x, conv_bc, dt_bias, a_log):
    length, inner = x_in.shape
    heads = dt_in.shape[1]
    width = inner + 2 * STATE
    return pl.pallas_call(
        conv_states_kernel,
        out_shape=(
            jax.ShapeDtypeStruct((length, width), BF16),
            jax.ShapeDtypeStruct((length, heads), F32),
            jax.ShapeDtypeStruct((heads, length), F32),
            jax.ShapeDtypeStruct((STATE, inner), BF16),
            jax.ShapeDtypeStruct((STATE, inner), BF16),
            jax.ShapeDtypeStruct((16, inner), BF16),
        ),
        in_specs=[VMEM] * 9,
        out_specs=(VMEM,) * 6,
        scratch_shapes=[pltpu.VMEM((length + 8, width), F32)],
        compiler_params=params(16),
        cost_estimate=pl.CostEstimate(flops=10**8, bytes_accessed=10**7, transcendentals=10**6),
    )(halo, x_in, b_in, c_in, dt_in.T, conv_x, conv_bc, dt_bias[None], a_log[None])


def diagonal(xbc, cum, back, first, d_skip):
    length = xbc.shape[0]
    inner = first.shape[1]
    return pl.pallas_call(
        diagonal_kernel,
        out_shape=jax.ShapeDtypeStruct((length, inner), F32),
        in_specs=[VMEM] * 4 + [SMEM],
        out_specs=VMEM,
        compiler_params=params(16),
        cost_estimate=pl.CostEstimate(flops=10**9, bytes_accessed=10**7, transcendentals=10**6),
    )(xbc, cum, back, first, d_skip)


def finish(acc, xbc, cum, z_in, came, gain):
    length, inner = acc.shape
    return pl.pallas_call(
        finish_kernel,
        out_shape=jax.ShapeDtypeStruct((length, inner), BF16),
        in_specs=[VMEM] * 3 + [HBM] + [VMEM] * (1 + len(came)),
        out_specs=VMEM,
        scratch_shapes=[
            pltpu.VMEM((128, inner), F32),
            pltpu.VMEM((length, inner), BF16),
            pltpu.SemaphoreType.DMA((1,)),
        ],
        compiler_params=params(16),
        cost_estimate=pl.CostEstimate(flops=10**9, bytes_accessed=10**7, transcendentals=10**6),
    )(acc, xbc, cum, z_in, gain, *came)


def decay_of(msg):
    return msg[STATE : STATE + 1].astype(F32) + msg[STATE + 8 : STATE + 9].astype(F32)


def joined(earlier, later):
    decay = decay_of(later)
    state = later[:STATE].astype(F32) + decay * earlier[:STATE].astype(F32)
    both = decay_of(earlier) * decay
    high = both.astype(BF16)
    low = (both - high.astype(F32)).astype(BF16)
    wide = (8, state.shape[1])
    return jnp.concatenate(
        [state.astype(BF16), jnp.broadcast_to(high, wide), jnp.broadcast_to(low, wide)], 0
    )


def hop(block, distance):
    count = lax.axis_size("ctx")
    return lax.ppermute(block, "ctx", [(i, i + distance) for i in range(count - distance)])


def extend_kernel(near_ref, state_ref, decay_ref, out_ref):
    decay = decay_ref[0:1].astype(F32) + decay_ref[8:9].astype(F32)
    out_ref[...] = (
        state_ref[...].astype(F32) + decay * near_ref[...].astype(F32)
    ).astype(BF16)


def extend(near, state, decay):
    return pl.pallas_call(
        extend_kernel,
        out_shape=jax.ShapeDtypeStruct(state.shape, BF16),
        in_specs=[VMEM] * 3,
        out_specs=VMEM,
        compiler_params=params(4),
        cost_estimate=pl.CostEstimate(flops=10**5, bytes_accessed=10**6, transcendentals=0),
    )(near, state, decay)


def chained(state, decay):
    came = []
    current = state
    for step in range(1, lax.axis_size("ctx")):
        came.append(line(current, (step - 1,), 1))
        if step + 1 < lax.axis_size("ctx"):
            current = extend(came[-1], state, decay)
    return came


def doubled(state, decay):
    count = lax.axis_size("ctx")
    msg = jnp.concatenate([state, decay], 0)
    near = hop(msg, 1)
    run, prior, reach = joined(near, msg), near, 2
    while reach < count:
        came = hop(run, reach)
        prior = joined(came, prior)
        run = joined(came, run)
        reach *= 2
    return [prior[:STATE]]


def swap_y(block, places, count):
    route = [(y * count + z, (1 - y) * count + z) for y in range(2) for z in places]
    return lax.ppermute(block, ("groups", "ctx"), route)


def line(block, sources, distance):
    return lax.ppermute(block, "ctx", [(i, i + distance) for i in sources])


def across(block, route):
    return lax.ppermute(block, "tp", route)


def fast_shards(*args):
    return fast_layer(*args)


def fast_layer(
    x_in, z_in, b_in, c_in, dt_in, conv_x, conv_bc, dt_bias, a_log, d_skip, norm_gain, out_weight
):
    count = 4
    rows = out_weight.shape[0]
    half = rows // 2
    part = FAR_ROWS
    rest = half - part
    place = jnp.stack(
        [lax.axis_index("ctx"), lax.axis_index("tp"), lax.axis_index("groups"), jnp.int32(count)]
    ).astype(jnp.int32)
    side = lax.axis_index("groups")[None].astype(jnp.int32)
    rim, head, rear = prepare(side, x_in, b_in, c_in, out_weight, part)
    other, rest_far = prepare_more(side, out_weight, rest)
    halo = hop(rim, 1)
    r1a = line(head, (0, 1, 2), 1)
    l1a = line(head, (1, 2, 3), -1)
    r1b = line(rear, (0, 1, 2), 1)
    l1b = line(rear, (1, 2, 3), -1)
    full = lax.ppermute(other, "ctx", ((0, 1), (3, 2)))
    r2a = line(r1a, (1,), 1)
    r2c = line(r1a, (2,), 1)
    l2a = line(l1a, (1, 2), -1)
    r2b = line(r1b, (1, 2), 1)
    l2b = line(l1b, (1, 2), -1)
    everywhere = (0, 1, 2, 3)
    y1a = swap_y(pick(place, (r1a, (2, 3)), (l1a, (0, 1))), everywhere, count)
    y1b = swap_y(pick(place, (r1b, (2, 3)), (l1b, (0, 1))), everywhere, count)
    head2 = pick(place, (r2a, (2,)), (r2c, (3,)), (l2a, (0, 1)))
    y2a = swap_y(head2, everywhere, count)
    y2b = swap_y(pick(place, (r2b, (2, 3)), (l2b, (0, 1))), everywhere, count)
    far = lax.ppermute(head2, "ctx", ((2, 3), (1, 0)))
    y3 = swap_y(far, (0, 3), count)
    db = lax.ppermute(rest_far, "ctx", ((0, 3), (3, 0)))

    normed = mixer(
        halo, x_in, z_in, b_in, c_in, dt_in, conv_x, conv_bc, dt_bias, a_log, d_skip, norm_gain
    )
    over = across(normed, ((0, 2), (2, 0), (1, 3), (3, 1)))
    core = ((0, 1), (1, 0), (2, 3), (3, 2))
    mate = across(normed, core)
    over_mate = across(over, core)
    all_normed = [normed, mate, over, over_mate]
    own_weight = in_hbm(out_weight)
    own = (0, 0, (0, 1, 2, 3), ((0, 0, rows, 0, 0),))

    def halves(slot, offset, places, head, rear, swapped):
        near = ((head, 0, part, 0, half), (rear, 0, rest, part, half + part))
        return (slot, offset, places, near + swapped)

    def swapped(first, second):
        return ((first, 0, part, half, 0), (second, 0, rest, half + part, part))

    total = product(
        place, all_normed, [own_weight, r1a, r1b, l1a, l1b, y1a, y1b],
        (
            own,
            halves(1, -1, (2, 3), 1, 2, swapped(5, 6)),
            halves(1, 1, (0, 1), 3, 4, swapped(5, 6)),
        ),
        None, False,
    )
    total = product(
        place, all_normed,
        [r1a, r1b, l1a, l1b, full, r2a, r2b, l2a, l2b, y2a, y2b, r2c],
        (
            halves(0, -1, (1,), 0, 1, ((4, 0, half, half, 0),)),
            halves(0, 1, (2,), 2, 3, ((4, 0, half, half, 0),)),
            halves(1, -2, (2,), 5, 6, swapped(9, 10)),
            halves(1, -2, (3,), 11, 6, swapped(9, 10)),
            halves(1, 2, (0, 1), 7, 8, swapped(9, 10)),
        ),
        total, False,
    )
    return product(
        place, all_normed, [far, y3, db],
        (
            (0, None, (0, 3), (
                (0, 0, part, 0, half),
                (1, 0, part, half, 0),
                (2, 0, rest, part, part),
                (2, rest, rest, half + part, half + part),
            )),
        ),
        total, True,
    )


def mixer(halo, x_in, z_in, b_in, c_in, dt_in, conv_x, conv_bc, dt_bias, a_log, d_skip, norm_gain):
    xbc, cum, back, first, state, decay = conv_states(
        x_in, b_in, c_in, halo, dt_in, conv_x, conv_bc, dt_bias, a_log
    )
    came = (chained if lax.axis_size("ctx") <= 4 else doubled)(state, decay)
    acc = diagonal(xbc, cum, back, first, d_skip)
    return finish(acc, xbc, cum, z_in, came, norm_gain[None])


def plain_shards(*args):
    out_weight = args[-1]
    weight = lax.all_gather(out_weight, "ctx", axis=0, tiled=True)
    x_in, _, b_in, c_in = args[:4]
    tail = x_in.shape[0] - 8
    halo = hop(jnp.concatenate([x_in[tail:], b_in[tail:], c_in[tail:]], 1), 1)
    normed = mixer(halo, *args[:-1])
    gathered = lax.all_gather(normed, "tp", axis=1, tiled=True)
    return jnp.dot(gathered, weight, preferred_element_type=F32).astype(BF16)


def solution(mesh):
    sizes = dict(mesh.shape)
    fast = sizes["groups"] == 2 and sizes["ctx"] == 4 and sizes["tp"] == 4
    return jax.shard_map(
        fast_shards if fast else plain_shards,
        mesh=mesh,
        in_specs=(
            P(("groups", "ctx"), "tp"),
            P(("groups", "ctx"), "tp"),
            P(("groups", "ctx"), "tp"),
            P(("groups", "ctx"), "tp"),
            P(("groups", "ctx"), "tp"),
            P(None, "tp"),
            P(None, None, "tp"),
            P("tp"),
            P("tp"),
            P("tp"),
            P("tp"),
            P("ctx", "tp"),
        ),
        out_specs=P(("groups", "ctx"), "tp"),
        check_vma=False,
    )
```
